32 devices in a mesh: node: 8 (over z, x), mp: 4 (over y, core).
Axes of the slice: x: 2, y: 2, z: 4, core: 2. Of those that a mesh axis runs over, the one named last changes fastest.
Arguments:
- queries: bfloat16 [32, 64, 128], P('node', 'mp'), may hold values from -8 to 8
- root_keys: bfloat16 [16384, 8, 128], P('node', 'mp'), may hold values from -6 to 6
- root_values: bfloat16 [16384, 8, 128], P('node', 'mp'), may hold values from -6 to 6
- mid_keys: bfloat16 [8, 1024, 8, 128], P('node', None, 'mp'), may hold values from -6 to 6
- mid_values: bfloat16 [8, 1024, 8, 128], P('node', None, 'mp'), may hold values from -6 to 6
- leaf_keys: bfloat16 [32, 256, 8, 128], P('node', None, 'mp'), may hold values from -6 to 6
- leaf_values: bfloat16 [32, 256, 8, 128], P('node', None, 'mp'), may hold values from -6 to 6
- mid_length: int32 [8], replicated, may hold values from 1 to 1024
- leaf_length: int32 [32], P('node'), may hold values from 1 to 256
- branch_mid: int32 [32, 1], replicated, may hold values from 0 to 7; in each aligned block of 32 rows (0 to 31, 32 to 63, ...) at most 8 rows name the same one
- residual: bfloat16 [32, 8192], P(None, 'node'), may hold values from -6 to 6
- norm_gain: float32 [8192], P('node'), may hold values from 0.5 to 1.5
- out_weight: bfloat16 [8192, 8192], P('mp', 'node'), may hold values from -0.0625 to 0.0625
- gate_weight: bfloat16 [8192, 28672], P('node', 'mp'), may hold values from -0.0625 to 0.0625
- up_weight: bfloat16 [8192, 28672], P('node', 'mp'), may hold values from -0.0625 to 0.0625
- down_weight: bfloat16 [28672, 8192], P('mp', 'node'), may hold values from -0.03125 to 0.03125
Outputs:
- layer_out: bfloat16 [32, 8192], P('mp', 'node')
The draws below stay inside these ranges and needn't reach their ends.
Inputs may be any that keep to these rules, and one draw needn't show every extreme that they name: `branch_mid`: every inner tree node lies on the path of 1 to 8 branches, and some node on exactly 8.
All inputs are finite; a program needn't handle non-finite values.
Results may differ from the reference program's by a relative error of at most 0.015.
Values may be sent and summed in bfloat16 or wider, within the bound.
A program may use at most 128 MiB of HBM per device.

```python
import math
import jax
import jax.numpy as jnp
import numpy as np
from jax import lax

D = 8192
FF = 28672
QH = 64
KVH = 8
HD = 128
MID_LEN = 1024
LEAF = 256
ROOT = 16384
CAP = 8
BRANCHES = 32
MIDS = 8


def draw_queries(key, part):
    values = jnp.clip(jax.random.normal(jax.random.fold_in(key, 5), (BRANCHES, QH, HD), jnp.float32), -6.0, 6.0)
    return values.astype(jnp.bfloat16)


def draw_root_keys(key, part):
    values = jnp.clip(jax.random.normal(jax.random.fold_in(key, 9), (ROOT, KVH, HD), jnp.float32), -6.0, 6.0)
    return values.astype(jnp.bfloat16)


def touch_ends(values, own_key, smallest, largest):
    dims = values.shape
    place = [jax.random.randint(jax.random.fold_in(own_key, axis), (), 0, dims[axis]) for axis in range(len(dims))]
    values = values.at[tuple(place)].set(smallest)
    longest = dims.index(max(dims))
    place[longest] = (place[longest] + 1) % dims[longest]
    return values.at[tuple(place)].set(largest)


def block_scale(key, shape, split, low, largest):
    factor_of, own = 1.0, jax.random.fold_in(key, 6)
    for position, shards_of in split:
        draws = jnp.exp(jax.random.uniform(jax.random.fold_in(own, position), (shards_of,), jnp.float32, low / len(split), largest / len(split)))
        factor_of = factor_of * jnp.repeat(draws, shape[position] // shards_of).reshape([-1 if axis == position else 1 for axis in range(len(shape))])
    return factor_of


def assign_block(own_key, own, number, rows, number_of, top, limit, lean):
    ranking = jax.random.permutation(own_key, number_of)
    crowded, common = load_shares(number_of, rows * top, limit, lean, True), load_shares(number_of, rows * top, limit, lean, False)
    places = jnp.arange(number_of)

    def named(sizes, offset_by):
        used = int((sizes > 0).sum())
        fixed = max(1, used // 4)
        moved = fixed + (places - fixed + offset_by * (used - fixed)) % max(1, number_of - fixed)
        return jnp.zeros((number_of,), jnp.int32).at[ranking[jnp.where(places < fixed, places, moved)]].set(jnp.asarray(sizes, jnp.int32))

    sizes = jnp.where(number % 4 == 0, named(crowded, number // 4), named(common, number - number // 4 - 1))
    mixed = jax.random.permutation(jax.random.fold_in(own, 3), number_of)
    source_of, taker = mixed[0:number_of // 2 * 2:2], mixed[1:number_of // 2 * 2:2]
    slack = jnp.minimum(sizes[source_of] - 1, limit - sizes[taker]) // 2
    slack = jnp.where((source_of == ranking[0]) | (taker == ranking[0]) | (sizes[taker] == 0), 0, jnp.maximum(slack, 0))
    moved = jax.random.randint(jax.random.fold_in(own, 4), (number_of // 2,), 0, 1 << 20) % (slack + 1)
    sizes = sizes.at[source_of].add(-moved).at[taker].add(moved)
    labels = jnp.searchsorted(jnp.cumsum(sizes), jnp.arange(rows * top), side="right").astype(jnp.int32)
    grid = labels.reshape(top, rows).T
    grid = grid[jax.random.permutation(jax.random.fold_in(own, 1), rows)]
    offset_by = jax.random.randint(jax.random.fold_in(own, 2), (rows, 1), 0, top)
    return jnp.take_along_axis(grid, (jnp.arange(top)[None, :] + offset_by) % top, axis=1)


def load_shares(amount, total, limit, skew, full):
    portions = [(1 << 20) // math.isqrt(standing ** skew) + 1 for standing in range(1, amount + 1)]
    largest = limit if full else min(limit, max(-(-total // amount), total * portions[0] // sum(portions)))
    least = 1 if total - largest >= amount - 1 else 0
    counts, rest = [largest] + [least] * (amount - 1), total - largest - least * (amount - 1)
    while rest > 0:
        movable = [i for i in range(1, amount) if counts[i] < largest] or [i for i in range(1, amount) if counts[i] < limit]
        mass, budget = sum([portions[i] for i in movable]), rest
        for i in movable:
            addition = min(limit - counts[i], max(1, budget * portions[i] // mass), rest)
            counts[i] = counts[i] + addition
            rest = rest - addition
    return np.array(counts)


def scatter_about(key, dims, deviation, most, pieces=(), held_as=jnp.bfloat16):
    drawn = deviation * jax.random.normal(key, dims, jnp.float32)
    if pieces:
        drawn = drawn * block_scale(key, dims, pieces, -0.22, 0.18)
    return jnp.clip(drawn, -most, most).astype(held_as)


def setup_inputs(seed: int = 0) -> dict:
    key_of = jax.random.split(jax.random.key(seed), 17)
    queries = draw_queries(jax.random.fold_in(key_of[16], 71), 0)
    root_keys = draw_root_keys(jax.random.fold_in(key_of[16], 71), 0)
    root_values = scatter_about(key_of[2], (ROOT, KVH, HD), 1.0, 6.0, ((0, 8), (1, 4)))
    mid_keys = scatter_about(key_of[3], (MIDS, MID_LEN, KVH, HD), 1.0, 6.0, ((0, 8), (2, 4)))
    mid_values = scatter_about(key_of[4], (MIDS, MID_LEN, KVH, HD), 1.0, 6.0, ((0, 8), (2, 4)))
    leaf_keys = scatter_about(key_of[5], (BRANCHES, LEAF, KVH, HD), 1.0, 6.0, ((0, 8), (2, 4)))
    leaf_values = scatter_about(key_of[6], (BRANCHES, LEAF, KVH, HD), 1.0, 6.0, ((0, 8), (2, 4)))
    mid_length = touch_ends(jax.random.randint(key_of[7], (MIDS,), 1, MID_LEN + 1), jax.random.fold_in(key_of[7], 1), 1, MID_LEN).astype(jnp.int32)
    leaf_length = touch_ends(jax.random.randint(key_of[8], (BRANCHES,), 1, LEAF + 1), jax.random.fold_in(key_of[8], 1), 1, LEAF).astype(jnp.int32)
    branch_mid_keys = jax.random.split(jax.random.fold_in(key_of[9], 1), BRANCHES // BRANCHES)
    branch_mid_turns = jax.random.permutation(jax.random.fold_in(key_of[9], 3), BRANCHES // BRANCHES)
    branch_mid = jax.vmap(lambda own, number: assign_block(jax.random.fold_in(key_of[9], 2), own, number, BRANCHES, MIDS, 1, CAP, 2))(branch_mid_keys, branch_mid_turns).reshape((BRANCHES, 1))
    residual = scatter_about(key_of[10], (BRANCHES, D), 1.0, 6.0, ((1, 8),))
    norm_gain = jnp.clip(1.0 + 0.1 * jax.random.normal(key_of[11], (D,), jnp.float32), 0.5, 1.5)
    out_weight = scatter_about(key_of[12], (QH * HD, D), (QH * HD) ** -0.5, 0.0625, ((0, 4), (1, 8)))
    gate_weight = scatter_about(key_of[13], (D, FF), D ** -0.5, 0.0625, ((0, 8), (1, 4)))
    up_weight = scatter_about(key_of[14], (D, FF), D ** -0.5, 0.0625, ((0, 8), (1, 4)))
    down_weight = scatter_about(key_of[15], (FF, D), FF ** -0.5, 0.03125, ((0, 4), (1, 8)))
    return dict(queries=queries, root_keys=root_keys, root_values=root_values, mid_keys=mid_keys, mid_values=mid_values, leaf_keys=leaf_keys, leaf_values=leaf_values, mid_length=mid_length, leaf_length=leaf_length, branch_mid=branch_mid, residual=residual, norm_gain=norm_gain, out_weight=out_weight, gate_weight=gate_weight, up_weight=up_weight, down_weight=down_weight)


masked_score = -1e+30
norm_eps = 1e-05

def reference(queries, root_keys, root_values, mid_keys, mid_values, leaf_keys, leaf_values, mid_length, leaf_length, branch_mid, residual, norm_gain, out_weight, gate_weight, up_weight, down_weight):
    group_size = QH // KVH
    scaling = 1.0 / math.sqrt(HD)

    def attend(inputs):
        query_rows, mid_index, leaf_key, leaf_value, leaf_count = inputs
        key_block = jnp.concatenate([root_keys, mid_keys[mid_index], leaf_key], axis=0).astype(jnp.float32)
        value_block = jnp.concatenate([root_values, mid_values[mid_index], leaf_value], axis=0).astype(jnp.float32)
        mid_count = mid_length[mid_index]
        usable = jnp.concatenate([jnp.ones((ROOT,), dtype=bool), jnp.arange(MID_LEN) < mid_count, jnp.arange(LEAF) < leaf_count])
        grouped = query_rows.astype(jnp.float32).reshape(KVH, group_size, HD)
        scores = jnp.einsum('kgd,lkd->kgl', grouped, key_block, precision=lax.Precision.HIGHEST) * scaling
        scores = jnp.where(usable, scores, masked_score)
        highest = lax.optimization_barrier(jnp.max(scores, axis=-1, keepdims=True))
        weights = jnp.where(usable, jnp.exp(scores - highest), 0.0)
        rounded = weights.astype(jnp.bfloat16).astype(jnp.float32)
        weighted = jnp.einsum('kgl,lkd->kgd', rounded, value_block, precision=lax.Precision.HIGHEST)
        return (weighted / lax.optimization_barrier(jnp.sum(weights, axis=-1))[..., None]).reshape(QH * HD)
    attended = lax.map(attend, (queries, branch_mid[:, 0], leaf_keys, leaf_values, leaf_length)).astype(jnp.bfloat16)
    stream = residual.astype(jnp.float32) + jnp.dot(attended, out_weight, preferred_element_type=jnp.float32)
    mean_square = lax.optimization_barrier(jnp.sum(stream * stream, axis=1, keepdims=True)) / D
    normed = (stream * lax.rsqrt(mean_square + norm_eps) * norm_gain[None, :]).astype(jnp.bfloat16)
    gate = jnp.dot(normed, gate_weight, preferred_element_type=jnp.float32)
    upward = jnp.dot(normed, up_weight, preferred_element_type=jnp.float32)
    act = (jax.nn.silu(gate) * upward).astype(jnp.bfloat16)
    return (stream + jnp.dot(act, down_weight, preferred_element_type=jnp.float32)).astype(jnp.bfloat16)
```

```python
import functools
import math

import jax
import jax.numpy as jnp
import numpy as np
from jax import lax
from jax.experimental import pallas as pl
from jax.experimental.pallas import tpu as pltpu
from jax.sharding import PartitionSpec as P

norm_eps = 1e-05
masked_score = -1e30
MESH = pl.DeviceIdType.MESH
ROWS = 128


def nt_dot(a, b):
    return lax.dot_general(a, b, (((1,), (1,)), ((), ())), preferred_element_type=jnp.float32)


def nn_dot(a, b):
    return jnp.dot(a, b, preferred_element_type=jnp.float32)


def layer_kernel(
    n, mp, owners, scale2,
    q_ref, mid_lo, mid_hi, leaf_lo, leaf_hi, spread_ref, order_ref, res_ref, gain_ref,
    rk_hbm, rv_hbm, mk_hbm, mv_hbm, lk_hbm, lv_hbm, ow_hbm, gw_hbm, uw_hbm, dw_hbm,
    out_ref,
    raw, keys, values, ow, gw, uw, dw,
    qall, part_send, part_recv, leaf_part, att_own, att_all, lhs, pr_own, pr_all, stream,
    sq_own, sq_all, xg, gu_send, gu_recv, act_all, acc, dn_send, dn_recv,
    kv_sem, w_sem, q_s, q_r, p_s, p_r, a_s, a_r, s_s, s_r, g_s, g_r, c_s, c_r, o_s, o_r, d_s, d_r,
):
    me = lax.axis_index("node")
    mpi = lax.axis_index("mp")
    heads, own_rows, hd = q_ref.shape
    chunk = act_all.shape[2]
    width = stream.shape[1]
    root = rk_hbm.shape[0] // heads
    mids = mk_hbm.shape[0] // heads
    leaves = lk_hbm.shape[0] // heads
    shared = root + mids

    kv_copies = []
    for side, (a, b, c) in enumerate(((rk_hbm, mk_hbm, lk_hbm), (rv_hbm, mv_hbm, lv_hbm))):
        start = 0
        for k, src in enumerate((a, b, c)):
            size = src.shape[0]
            copy = pltpu.make_async_copy(
                src, raw.at[side, pl.ds(start, size)], kv_sem.at[side * 3 + k]
            )
            copy.start()
            kv_copies.append(copy)
            start += size
    w_copies = []
    for k, (src, dst) in enumerate(((ow_hbm, ow), (gw_hbm, gw), (uw_hbm, uw), (dw_hbm, dw))):
        copy = pltpu.make_async_copy(src, dst, w_sem.at[k])
        copy.start()
        w_copies.append(copy)

    barrier = pltpu.get_barrier_semaphore()

    def greet(axis, here, count):
        def body(i, carry):
            pl.semaphore_signal(
                barrier, inc=1, device_id={axis: lax.rem(here + i, count)}, device_id_type=MESH
            )
            return carry

        lax.fori_loop(1, count, body, 0)

    greet("node", me, n)
    greet("mp", mpi, mp)
    pl.semaphore_wait(barrier, n - 1 + mp - 1)

    def remote(src, dst, send, recv, axis, peer):
        return pltpu.make_async_remote_copy(
            src_ref=src, dst_ref=dst, send_sem=send, recv_sem=recv,
            device_id={axis: peer}, device_id_type=MESH,
        )

    def peers(axis, fn):
        here, count = (me, n) if axis == "node" else (mpi, mp)

        def body(i, carry):
            fn(lax.rem(here + i, count))
            return carry

        lax.fori_loop(1, count, body, 0)

    def send_all(axis, src, dst, send, recv):
        here = me if axis == "node" else mpi
        peers(
            axis,
            lambda j: remote(src(j), dst.at[here], send.at[j], recv.at[here], axis, j).start(),
        )

    def wait_all(axis, src, dst, send, recv):
        peers(axis, lambda j: remote(src(j), dst.at[j], send.at[j], recv.at[j], axis, j).wait())

    send_all("node", lambda j: q_ref, qall, q_s, q_r)
    qall[me] = q_ref[...]

    for copy in kv_copies:
        copy.wait()
    block = spread_ref.shape[0]
    per = block // heads

    def split(i, carry):
        at = pl.ds(pl.multiple_of(i * block, block), block)
        to = pl.ds(pl.multiple_of(i * per, per), per)
        for side, dst in enumerate((keys, values)):
            rows = nn_dot(spread_ref[...], raw[side, at, :]).astype(jnp.bfloat16)
            for h in range(heads):
                dst[h, to, :] = rows[h * per:(h + 1) * per]
        return carry

    lax.fori_loop(0, raw.shape[1] // block, split, 0)

    def leaf_attend(h):
        scores = nt_dot(q_ref[h], keys[h, shared:, :])
        slot = lax.broadcasted_iota(jnp.int32, scores.shape, 1)
        seen = (slot >= leaf_lo[...]) & (slot < leaf_hi[...])
        scores = jnp.where(seen, scores, masked_score)
        peak = jnp.max(scores, axis=1, keepdims=True)
        weights = jnp.where(seen, jnp.exp2((scores - peak) * scale2), 0.0)
        total = jnp.sum(weights, axis=1, keepdims=True)
        weighted = nn_dot(weights.astype(jnp.bfloat16), values[h, shared:, :])
        lane = lax.broadcasted_iota(jnp.int32, (own_rows, hd), 1)
        leaf_part[h, :, 0:hd] = weighted
        leaf_part[h, :, hd:] = jnp.where(lane == 0, peak, total)

    for h in range(heads):
        leaf_attend(h)

    wait_all("node", lambda j: q_ref, qall, q_s, q_r)

    group = max(1, min(n, ROWS // own_rows))
    rows = group * own_rows

    def attend(i, carry):
        picks = pl.ds(i * group, group)
        at = pl.ds(pl.multiple_of(i * rows, rows), rows)
        low, high = mid_lo[at, :], mid_hi[at, :]
        for h in range(heads):
            query = qall[picks, h].reshape(rows, hd)
            root_scores = nt_dot(query, keys[h, 0:root, :])
            mid_scores = nt_dot(query, keys[h, root:shared, :])
            slot = lax.broadcasted_iota(jnp.int32, mid_scores.shape, 1)
            seen = (slot >= low) & (slot < high)
            mid_scores = jnp.where(seen, mid_scores, masked_score)
            peak = jnp.maximum(
                jnp.max(root_scores, axis=1, keepdims=True),
                jnp.max(mid_scores, axis=1, keepdims=True),
            )
            root_weights = jnp.exp2((root_scores - peak) * scale2)
            mid_weights = jnp.where(seen, jnp.exp2((mid_scores - peak) * scale2), 0.0)
            total = jnp.sum(root_weights, axis=1, keepdims=True) + jnp.sum(
                mid_weights, axis=1, keepdims=True
            )
            weighted = nn_dot(root_weights.astype(jnp.bfloat16), values[h, 0:root, :]) + nn_dot(
                mid_weights.astype(jnp.bfloat16), values[h, root:shared, :]
            )
            lane = lax.broadcasted_iota(jnp.int32, (rows, hd), 1)
            side = jnp.where(lane == 0, peak, total)
            part_send[picks, h, :, 0:hd] = weighted.reshape(group, own_rows, hd)
            part_send[picks, h, :, hd:] = side.reshape(group, own_rows, hd)
        return carry

    lax.fori_loop(0, n // group, attend, 0)
    send_all("node", lambda j: part_send.at[j], part_recv, p_s, p_r)
    part_recv[me] = part_send[me]
    wait_all("node", lambda j: part_send.at[j], part_recv, p_s, p_r)

    for h in range(heads):
        def merge(i, carry):
            peak, total, weighted = carry
            peak_i = part_recv[i, h, :, hd:hd + 1]
            total_i = part_recv[i, h, :, hd + 1:hd + 2]
            top = jnp.maximum(peak, peak_i)
            one, two = jnp.exp2((peak - top) * scale2), jnp.exp2((peak_i - top) * scale2)
            return (
                top,
                total * one + total_i * two,
                weighted * one + part_recv[i, h, :, 0:hd] * two,
            )

        first = (
            leaf_part[h, :, hd:hd + 1],
            leaf_part[h, :, hd + 1:hd + 2],
            leaf_part[h, :, 0:hd],
        )
        _, total, weighted = lax.fori_loop(0, n, merge, first)
        att_own[h] = (weighted / total).astype(jnp.bfloat16)

    send_all("node", lambda j: att_own, att_all, a_s, a_r)
    att_all[me] = att_own[...]
    wait_all("node", lambda j: att_own, att_all, a_s, a_r)

    branches = lhs.shape[0]
    size = n * own_rows // branches
    for h in range(heads):
        mixed = att_all[:, h].reshape(n * own_rows, hd)
        mixed = nn_dot(order_ref[...], mixed).astype(jnp.bfloat16)
        for g in range(size):
            first = (h * size + g) * hd
            lhs[:, first:first + hd] = mixed[g * branches:(g + 1) * branches]

    w_copies[0].wait()
    tile = math.gcd(width, 256)

    def project(i, carry):
        at = pl.ds(pl.multiple_of(i * tile, tile), tile)
        pr_own[:, at] = nn_dot(lhs[...], ow[:, at]).astype(jnp.bfloat16)
        return carry

    lax.fori_loop(0, width // tile, project, 0)
    send_all("mp", lambda j: pr_own, pr_all, o_s, o_r)
    pr_all[mpi] = pr_own[...]
    wait_all("mp", lambda j: pr_own, pr_all, o_s, o_r)
    total = pr_all[0].astype(jnp.float32)
    for k in range(1, mp):
        total = total + pr_all[k].astype(jnp.float32)
    total = res_ref[...].astype(jnp.float32) + total
    stream[...] = total
    squares = jnp.sum(total * total, axis=1, keepdims=True)
    sq_own[...] = jnp.broadcast_to(squares, sq_own.shape)
    send_all("node", lambda j: sq_own, sq_all, s_s, s_r)
    sq_all[me] = sq_own[...]
    xg[...] = (total * gain_ref[...]).astype(jnp.bfloat16)

    w_copies[1].wait()
    w_copies[2].wait()

    def gate_up(i, carry):
        j = lax.rem(me + 1 + i, owners)
        at = pl.ds(pl.multiple_of(j * chunk, 128), chunk)
        gate = nn_dot(xg[...], gw[:, at]).astype(jnp.bfloat16)
        upward = nn_dot(xg[...], uw[:, at]).astype(jnp.bfloat16)
        gu_send[j, 0] = gate
        gu_send[j, 1] = upward

        @pl.when(j != me)
        def _():
            remote(gu_send.at[j], gu_recv.at[me], g_s.at[j], g_r.at[me], "node", j).start()

        return carry

    lax.fori_loop(0, owners, gate_up, 0)
    wait_all("node", lambda j: sq_own, sq_all, s_s, s_r)

    def owner_work():
        gu_recv[me] = gu_send[me]
        peers(
            "node",
            lambda j: remote(gu_send.at[0], gu_recv.at[j], g_s.at[0], g_r.at[j], "node", j).wait_recv(),
        )
        squares = sq_all[0][:, 0:1]
        for k in range(1, n):
            squares = squares + sq_all[k][:, 0:1]
        root_mean = lax.rsqrt(squares / (width * n) + norm_eps)

        def add(i, carry):
            return (
                carry[0] + gu_recv[i, 0].astype(jnp.float32),
                carry[1] + gu_recv[i, 1].astype(jnp.float32),
            )

        zero = jnp.zeros((branches, chunk), jnp.float32)
        gate, upward = lax.fori_loop(0, n, add, (zero, zero))
        gate, upward = gate * root_mean, upward * root_mean
        act_all[me] = (gate / (1.0 + jnp.exp(-gate)) * upward).astype(jnp.bfloat16)
        send_all("node", lambda j: act_all.at[me], act_all, c_s, c_r)

    if owners == n:
        owner_work()
    else:
        pl.when(me < owners)(owner_work)

    w_copies[3].wait()
    acc[...] = jnp.zeros(acc.shape, jnp.float32)

    def down(i, carry):
        j = lax.rem(me + i, n)

        def step():
            @pl.when(j != me)
            def _():
                remote(act_all.at[j], act_all.at[j], c_s.at[j], c_r.at[j], "node", j).wait_recv()

            at = pl.ds(pl.multiple_of(j * chunk, 128), chunk)
            acc[...] += nn_dot(act_all[j], dw[at, :])

        if owners == n:
            step()
        else:
            pl.when(j < owners)(step)
        return carry

    lax.fori_loop(0, n, down, 0)

    rows_out = out_ref.shape[0]
    for k in range(mp):
        dn_send[k] = acc[k * rows_out:(k + 1) * rows_out, :].astype(jnp.bfloat16)
    send_all("mp", lambda j: dn_send.at[j], dn_recv, d_s, d_r)
    dn_recv[mpi] = dn_send[mpi]
    wait_all("mp", lambda j: dn_send.at[j], dn_recv, d_s, d_r)
    total = dn_recv[0].astype(jnp.float32)
    for k in range(1, mp):
        total = total + dn_recv[k].astype(jnp.float32)
    own = stream[pl.ds(pl.multiple_of(mpi * rows_out, rows_out), rows_out), :]
    out_ref[...] = (own + total).astype(jnp.bfloat16)

    def sent(i, carry):
        j = lax.rem(me + 1 + i, owners)

        @pl.when(j != me)
        def _():
            remote(gu_send.at[j], gu_recv.at[me], g_s.at[j], g_r.at[me], "node", j).wait_send()

        return carry

    lax.fori_loop(0, owners, sent, 0)

    def acts_sent():
        peers(
            "node",
            lambda j: remote(act_all.at[me], act_all.at[me], c_s.at[j], c_r.at[j], "node", j).wait_send(),
        )

    if owners == n:
        acts_sent()
    else:
        pl.when(me < owners)(acts_sent)


def on_device(
    n, mp,
    queries, root_keys, root_values, mid_keys, mid_values, leaf_keys, leaf_values,
    mid_length, leaf_length, branch_mid, residual, norm_gain,
    out_weight, gate_weight, up_weight, down_weight,
):
    owned, local_heads, hd = queries.shape
    heads = root_keys.shape[1]
    size = local_heads // heads
    own_rows = owned * size
    branches = owned * n
    width = residual.shape[1]
    hidden = gate_weight.shape[1]
    lane_tiles = hidden // 128
    owners = max(k for k in range(1, n + 1) if lane_tiles % k == 0)
    chunk = hidden // owners
    mid_slots = mid_keys.shape[1]
    leaf_slots = leaf_keys.shape[1]
    local_mids = mid_keys.shape[0]

    q = queries.reshape(owned, heads, size, hd).transpose(1, 0, 2, 3).reshape(heads, own_rows, hd)
    local = branch_mid[:, 0] - lax.axis_index("node") * local_mids
    here = (local >= 0) & (local < local_mids)
    mid_lo = jnp.where(here, local * mid_slots, 0)
    mid_hi = jnp.where(here, mid_lo + mid_length[branch_mid[:, 0]], 0)
    mid_lo = jnp.repeat(mid_lo, size)[:, None]
    mid_hi = jnp.repeat(mid_hi, size)[:, None]
    leaf_lo = jnp.arange(owned, dtype=jnp.int32) * leaf_slots
    leaf_hi = jnp.repeat(leaf_lo + leaf_length, size)[:, None]
    leaf_lo = jnp.repeat(leaf_lo, size)[:, None]

    block = 128 * heads
    spread = np.zeros((block, block), np.float32)
    at = np.arange(block)
    spread[(at % heads) * 128 + at // heads, at] = 1.0
    order = np.zeros((branches * size, branches * size), np.float32)
    at = np.arange(branches * size)
    order[(at % size) * branches + at // size, at] = 1.0

    flat = [
        a.reshape(-1, hd)
        for a in (root_keys, root_values, mid_keys, mid_values, leaf_keys, leaf_values)
    ]
    raw_rows = flat[0].shape[0] + flat[2].shape[0] + flat[4].shape[0]
    bf, f32 = jnp.bfloat16, jnp.float32
    dma = pltpu.SemaphoreType.DMA
    vmem = pl.BlockSpec(memory_space=pltpu.VMEM)
    hbm = pl.BlockSpec(memory_space=pl.ANY)
    rows_out = branches // mp
    scratch = [
        pltpu.VMEM((2, raw_rows, hd), bf),
        pltpu.VMEM((heads, raw_rows // heads, hd), bf),
        pltpu.VMEM((heads, raw_rows // heads, hd), bf),
        pltpu.VMEM(out_weight.shape, bf),
        pltpu.VMEM(gate_weight.shape, bf),
        pltpu.VMEM(up_weight.shape, bf),
        pltpu.VMEM(down_weight.shape, bf),
        pltpu.VMEM((n, heads, own_rows, hd), bf),
        pltpu.VMEM((n, heads, own_rows, 2 * hd), f32),
        pltpu.VMEM((n, heads, own_rows, 2 * hd), f32),
        pltpu.VMEM((heads, own_rows, 2 * hd), f32),
        pltpu.VMEM((heads, own_rows, hd), bf),
        pltpu.VMEM((n, heads, own_rows, hd), bf),
        pltpu.VMEM((branches, local_heads * hd), bf),
        pltpu.VMEM((branches, width), bf),
        pltpu.VMEM((mp, branches, width), bf),
        pltpu.VMEM((branches, width), f32),
        pltpu.VMEM((branches, 128), f32),
        pltpu.VMEM((n, branches, 128), f32),
        pltpu.VMEM((branches, width), bf),
        pltpu.VMEM((owners, 2, branches, chunk), bf),
        pltpu.VMEM((n, 2, branches, chunk), bf),
        pltpu.VMEM((owners, branches, chunk), bf),
        pltpu.VMEM((branches, width), f32),
        pltpu.VMEM((mp, rows_out, width), bf),
        pltpu.VMEM((mp, rows_out, width), bf),
        dma((6,)),
        dma((4,)),
    ] + [dma((n,))] * 12 + [dma((mp,))] * 4
    scale2 = hd ** -0.5 * math.log2(math.e)
    return pl.pallas_call(
        functools.partial(layer_kernel, n, mp, owners, scale2),
        out_shape=jax.ShapeDtypeStruct((rows_out, width), bf),
        in_specs=[vmem] * 9 + [hbm] * 10,
        out_specs=vmem,
        scratch_shapes=scratch,
        compiler_params=pltpu.CompilerParams(
            collective_id=0, has_side_effects=True, vmem_limit_bytes=67043328
        ),
    )(
        q, mid_lo, mid_hi, leaf_lo, leaf_hi,
        jnp.asarray(spread, bf), jnp.asarray(order, bf), residual, norm_gain[None, :],
        *flat, out_weight, gate_weight, up_weight, down_weight,
    )


def solution(mesh):
    in_specs = (
        P("node", "mp", None),
        P("node", "mp", None),
        P("node", "mp", None),
        P("node", None, "mp", None),
        P("node", None, "mp", None),
        P("node", None, "mp", None),
        P("node", None, "mp", None),
        P(),
        P("node"),
        P(),
        P(None, "node"),
        P("node"),
        P("mp", "node"),
        P("node", "mp"),
        P("node", "mp"),
        P("mp", "node"),
    )
    body = functools.partial(on_device, mesh.shape["node"], mesh.shape["mp"])
    return jax.shard_map(
        body, mesh=mesh, in_specs=in_specs, out_specs=P("mp", "node"), check_vma=False
    )
```
